256 devices in a mesh: dp: 4 (over x), seq: 64 (over z, y, core).
Axes of the slice: x: 4, y: 4, z: 8, core: 2. Of those that a mesh axis runs over, the one named last changes fastest.
Arguments:
- query_gate: bfloat16 [4, 8192, 4096], P('dp', 'seq'), may hold values from -6 to 6
- key_gate: bfloat16 [4, 8192, 4096], P('dp', 'seq'), may hold values from -6 to 6
- value_feat: bfloat16 [4, 8192, 4096], P('dp', 'seq'), may hold values from -6 to 6
- filters: bfloat16 [256, 128], replicated, may hold values from -0.5 to 0.5
- grad_out: bfloat16 [4, 8192, 4096], P('dp', 'seq'), may hold values from -6 to 6
- basis_prev: float32 [128, 16], replicated, may hold values from -6 to 6
Outputs:
- mixed_out: bfloat16 [4, 8192, 4096], P('dp', 'seq')
- grad_query: bfloat16 [4, 8192, 4096], P('dp', 'seq')
- grad_key: bfloat16 [4, 8192, 4096], P('dp', 'seq')
- grad_value: bfloat16 [4, 8192, 4096], P('dp', 'seq')
- low_rank_grad: float32 [256, 128], replicated
- basis_next: float32 [128, 16], replicated
The draws below stay inside these ranges and needn't reach their ends.
All inputs are finite; a program needn't handle non-finite values.
Results may differ from the reference program's by a relative error of at most 0.0061.
Values may be sent and summed in bfloat16 or wider, within the bound.
No kernel may reach another device: no remote copies, remote signals or barrier semaphores. Data moves between devices by JAX's collectives and lax.ppermute only.
A program may use at most 192 MiB of HBM per device.

```python
import jax
import jax.numpy as jnp
from jax import lax

CHANNELS = 4096
GROUP = 16
TAPS = 128
RANK = 16
GROUPS = 256
BATCH = 4
SEQ_LEN = 8192


def shard_levels(stream_key, dims, shards, smallest, largest):
    loudness = 1.0
    for position, shards_of in shards:
        heights = jax.random.uniform(jax.random.fold_in(jax.random.fold_in(stream_key, 6), position), (shards_of,), jnp.float32, smallest / len(shards), largest / len(shards))
        loudness = loudness * jnp.repeat(jnp.exp(heights), dims[position] // shards_of).reshape((-1,) + (1,) * (len(dims) - 1 - position))
    return loudness


def bell_draw(stream_key, extent, deviation, bound, shards=(), kind=jnp.bfloat16):
    values = jax.random.normal(stream_key, extent, jnp.float32) * deviation
    if len(shards) > 0:
        values = shard_levels(stream_key, extent, shards, -0.22, 0.18) * values
    return jnp.clip(values, min=-bound, max=bound).astype(kind)


def setup_inputs(seed: int = 0) -> dict:
    streams_of = jax.random.split(jax.random.key(seed), 7)
    return {
        "query_gate": bell_draw(streams_of[0], (BATCH, SEQ_LEN, CHANNELS), 1.0, 6.0, ((0, 4), (1, 64))),
        "key_gate": bell_draw(streams_of[1], (BATCH, SEQ_LEN, CHANNELS), 1.0, 6.0, ((0, 4), (1, 64))),
        "value_feat": bell_draw(streams_of[2], (BATCH, SEQ_LEN, CHANNELS), 1.0, 6.0, ((0, 4), (1, 64))),
        "filters": bell_draw(streams_of[3], (GROUPS, TAPS), TAPS ** -0.5, 0.5),
        "grad_out": bell_draw(streams_of[4], (BATCH, SEQ_LEN, CHANNELS), 1.0, 6.0, ((0, 4), (1, 64))),
        "basis_prev": bell_draw(streams_of[5], (TAPS, RANK), 1.0, 6.0, (), jnp.float32),
    }


def orthonormal(left):
    columns = []
    for index in range(left.shape[1]):
        column = left[:, index]
        if index > 0:
            basis = jnp.stack(columns, axis=1)
            coeffs = jnp.dot(basis.T, column, precision=lax.Precision.HIGHEST)
            column = column - jnp.dot(basis, coeffs, precision=lax.Precision.HIGHEST)
        columns.append(column / jnp.sqrt(jnp.sum(column * column) + 1e-06))
    return jnp.stack(columns, axis=1)

def reference(query_gate, key_gate, value_feat, filters, grad_out, basis_prev):
    product = (key_gate.astype(jnp.float32) * value_feat.astype(jnp.float32)).astype(jnp.bfloat16)
    grad_conv = (grad_out.astype(jnp.float32) * query_gate.astype(jnp.float32)).astype(jnp.bfloat16)
    length = SEQ_LEN + TAPS
    width_blk = min(256, CHANNELS)
    count = CHANNELS // width_blk
    per_chan = jnp.repeat(filters.astype(jnp.float32), GROUP, axis=0)

    def one_block(index):
        start = index * width_blk
        piece_s = lax.dynamic_slice_in_dim(product, start, width_blk, 2).astype(jnp.float32)
        piece_d = lax.dynamic_slice_in_dim(grad_conv, start, width_blk, 2).astype(jnp.float32)
        piece_h = lax.dynamic_slice_in_dim(per_chan, start, width_blk, 0)
        spec_s = jnp.fft.rfft(piece_s, length, axis=1)
        spec_d = jnp.fft.rfft(piece_d, length, axis=1)
        spec_h = jnp.fft.rfft(piece_h.T, length, axis=0)[None]
        conv_b = jnp.fft.irfft(spec_s * spec_h, length, axis=1)[:, :SEQ_LEN]
        back_b = jnp.fft.irfft(spec_d * jnp.conj(spec_h), length, axis=1)[:, :SEQ_LEN]
        cross = jnp.fft.irfft(spec_d * jnp.conj(spec_s), length, axis=1)[:, :TAPS]
        cross = lax.optimization_barrier(jnp.sum(cross, axis=0)).reshape(TAPS, width_blk // GROUP, GROUP).sum(axis=2)
        return (conv_b.astype(jnp.float32), back_b.astype(jnp.float32), cross.T.astype(jnp.float32))
    conv_all, back_all, grad_rows = lax.map(one_block, jnp.arange(count, dtype=jnp.int32))
    conv = jnp.moveaxis(conv_all, 0, 2).reshape(BATCH, SEQ_LEN, CHANNELS)
    grad_product = jnp.moveaxis(back_all, 0, 2).reshape(BATCH, SEQ_LEN, CHANNELS)
    grad_filter = grad_rows.reshape(GROUPS, TAPS)
    mixed_out = (query_gate.astype(jnp.float32) * conv).astype(jnp.bfloat16)
    grad_query = (grad_out.astype(jnp.float32) * conv).astype(jnp.bfloat16)
    grad_key = (grad_product * value_feat.astype(jnp.float32)).astype(jnp.bfloat16)
    grad_value = (grad_product * key_gate.astype(jnp.float32)).astype(jnp.bfloat16)
    left = jnp.dot(grad_filter, basis_prev, precision=lax.Precision.HIGHEST)
    ortho = orthonormal(left)
    scale = (BATCH * SEQ_LEN * GROUP) ** (-0.5)
    basis_next = jnp.dot(grad_filter.T, ortho, precision=lax.Precision.HIGHEST) * scale
    low_rank_grad = jnp.dot(ortho, basis_next.T, precision=lax.Precision.HIGHEST)
    return (mixed_out, grad_query, grad_key, grad_value, low_rank_grad, basis_next)
```

```python
import functools

import jax
import jax.numpy as jnp
from jax import lax
from jax.experimental import pallas as pl
from jax.experimental.pallas import tpu as pltpu
from jax.sharding import Mesh
from jax.sharding import PartitionSpec as P

HIGH = lax.Precision.HIGHEST
LANES = 256
TILE = 16
WINDOW = 144
NT = (((1,), (1,)), ((), ()))
VMEM_LIMIT = 40 * 1024 * 1024


def lag_kernel(keep_ref, prod_ref, grad_ref, after_ref, mask_ref, flip_ref, out_ref):
    prod = jnp.dot(
        flip_ref[...], prod_ref[...], preferred_element_type=jnp.float32
    ).astype(jnp.bfloat16)
    after = after_ref[...] * keep_ref[0].astype(jnp.bfloat16)
    window = jnp.concatenate([grad_ref[...], after], axis=0)
    mask = mask_ref[...]
    tok = prod.shape[0]
    groups = LANES // TILE
    total = jnp.zeros((groups * TILE, WINDOW), jnp.float32)
    for low in range(0, tok, TILE):
        rows = jnp.concatenate([prod[low : low + TILE]] * groups, axis=0) * mask
        total += lax.dot_general(
            rows, window[low : low + WINDOW], NT, preferred_element_type=jnp.float32
        )
    wide = jnp.concatenate(
        [total, jnp.zeros((groups * TILE, LANES - WINDOW), jnp.float32)], axis=1
    ).reshape(groups, TILE, LANES)
    lined = jnp.sum(pltpu.roll(wide, 0, 2, stride=1, stride_axis=1), axis=1)
    out_ref[...] = pltpu.roll(lined, LANES - TILE + 1, 1)[:, : out_ref.shape[1]]


def lag_sums(keep, prod, grad, after, mask, flip, taps):
    tok, channels = prod.shape
    blocks = channels // LANES
    col = pl.BlockSpec((tok, LANES), lambda i: (0, i))
    return pl.pallas_call(
        lag_kernel,
        grid=(blocks,),
        in_specs=[
            pl.BlockSpec(memory_space=pltpu.SMEM),
            col,
            col,
            col,
            pl.BlockSpec((LANES, LANES), lambda i: (0, 0)),
            pl.BlockSpec((tok, tok), lambda i: (0, 0)),
        ],
        out_specs=pl.BlockSpec((TILE, taps), lambda i: (i, 0)),
        out_shape=jax.ShapeDtypeStruct((channels // TILE, taps), jnp.float32),
        compiler_params=pltpu.CompilerParams(vmem_limit_bytes=VMEM_LIMIT),
        cost_estimate=pl.CostEstimate(
            flops=2 * tok * channels * LANES * 16,
            bytes_accessed=6 * tok * channels,
            transcendentals=0,
        ),
        name="lag_sums",
    )(keep, prod, grad, after, mask, flip)


def conv_kernel(halo_first, keep_ref, line_ref, here_ref, halo_ref, a_ref, b_ref, x_ref, y_ref):
    groups = LANES // TILE
    halo = halo_ref[...] * keep_ref[0].astype(jnp.bfloat16)
    parts = [halo, here_ref[...]] if halo_first else [here_ref[...], halo]
    window = jnp.concatenate(parts, axis=0)
    line = line_ref[...]
    wide = jnp.broadcast_to(line[:, None, :], (groups, TILE, LANES))
    table = pltpu.roll(wide, 0, 2, stride=1, stride_axis=1)
    table = table.reshape(groups * TILE, LANES)[:, :WINDOW].astype(jnp.bfloat16)
    lane_group = lax.broadcasted_iota(jnp.int32, (TILE, 128), 1) // TILE
    for low in range(0, here_ref.shape[0], TILE):
        full = lax.dot_general(
            table,
            window[low : low + WINDOW],
            (((1,), (0,)), ((), ())),
            preferred_element_type=jnp.float32,
        )
        for half in range(LANES // 128):
            lanes = slice(half * 128, half * 128 + 128)
            conv = None
            for g in range(8):
                row = (half * 8 + g) * TILE
                mine = full[row : row + TILE, lanes]
                conv = mine if conv is None else jnp.where(lane_group == g, mine, conv)
            rows = slice(low, low + TILE)
            x_ref[rows, lanes] = (a_ref[rows, lanes].astype(jnp.float32) * conv).astype(jnp.bfloat16)
            y_ref[rows, lanes] = (b_ref[rows, lanes].astype(jnp.float32) * conv).astype(jnp.bfloat16)


def gated_conv(keep, line, here, halo, gate_a, gate_b, halo_first):
    tok, channels = here.shape
    blocks = channels // LANES
    col = pl.BlockSpec((tok, LANES), lambda i: (0, i))
    return pl.pallas_call(
        functools.partial(conv_kernel, halo_first),
        grid=(blocks,),
        in_specs=[
            pl.BlockSpec(memory_space=pltpu.SMEM),
            pl.BlockSpec((TILE, LANES), lambda i: (i, 0)),
            col,
            col,
            col,
            col,
        ],
        out_specs=[col, col],
        out_shape=[jax.ShapeDtypeStruct((tok, channels), jnp.bfloat16)] * 2,
        compiler_params=pltpu.CompilerParams(vmem_limit_bytes=VMEM_LIMIT),
        cost_estimate=pl.CostEstimate(
            flops=2 * tok * channels * LANES * 16,
            bytes_accessed=12 * tok * channels,
            transcendentals=0,
        ),
        name="conv_fwd" if halo_first else "conv_bwd",
    )(keep, line, here, halo, gate_a, gate_b)


def low_rank_kernel(scale, grad_ref, basis_ref, low_ref, next_ref):
    grad = grad_ref[...]
    rank = basis_ref.shape[1]
    left = lax.dot_general(
        basis_ref[...], grad, (((0,), (1,)), ((), ())), precision=HIGH,
        preferred_element_type=jnp.float32,
    )
    index = lax.broadcasted_iota(jnp.int32, left.shape, 0)
    rest = left
    ortho = jnp.zeros_like(left)
    for i in range(rank):
        row = rest[i : i + 1]
        unit = row / jnp.sqrt(jnp.sum(row * row, axis=1, keepdims=True) + 1e-06)
        ortho = jnp.where(index == i, unit, ortho)
        coeff = jnp.sum(left * unit, axis=1, keepdims=True)
        rest = rest - coeff * unit
    right = lax.dot_general(
        grad, ortho, (((0,), (1,)), ((), ())), precision=HIGH,
        preferred_element_type=jnp.float32,
    ) * scale
    next_ref[...] = right
    low_ref[...] = lax.dot_general(
        ortho, right, (((0,), (1,)), ((), ())), precision=HIGH,
        preferred_element_type=jnp.float32,
    )


def low_rank(grad, basis, scale):
    return pl.pallas_call(
        functools.partial(low_rank_kernel, scale),
        out_shape=[
            jax.ShapeDtypeStruct(grad.shape, jnp.float32),
            jax.ShapeDtypeStruct(basis.shape, jnp.float32),
        ],
        name="low_rank",
    )(grad, basis)


def summed(local):
    near = ("dp", "y", "core")
    rows = local.shape[0]
    count = lax.axis_size(near)
    piece = lax.all_to_all(local, near, 0, 0, tiled=True)
    piece = piece.reshape(count, rows // count, -1).sum(axis=0)
    size = lax.axis_size("z")
    step = 1
    while step < size:
        piece = piece + lax.ppermute(piece, "z", [(i, i ^ step) for i in range(size)])
        step *= 2
    spread = jnp.broadcast_to(piece[None], (count,) + piece.shape).reshape(rows, -1)
    return lax.all_to_all(spread, near, 0, 0, tiled=True)


def on_device(query_gate, key_gate, value_feat, filters, grad_out, basis_prev):
    gate_q, gate_k, feat_v, cotan = query_gate[0], key_gate[0], value_feat[0], grad_out[0]
    tok, channels = gate_q.shape
    groups, taps = filters.shape
    seq = ("z", "y", "core")
    size = lax.axis_size(seq)
    place = lax.axis_index(seq)
    product = (gate_k.astype(jnp.float32) * feat_v.astype(jnp.float32)).astype(jnp.bfloat16)
    grad_conv = (cotan.astype(jnp.float32) * gate_q.astype(jnp.float32)).astype(jnp.bfloat16)
    after = lax.ppermute(grad_conv, seq, [(i, (i - 1) % size) for i in range(size)])
    before = lax.ppermute(product, seq, [(i, (i + 1) % size) for i in range(size)])
    has_before = (place > 0).astype(jnp.float32)[None]
    has_after = (place < size - 1).astype(jnp.float32)[None]
    mask = (jnp.arange(LANES)[:, None] // TILE == jnp.arange(LANES)[None, :] // TILE)
    row = jnp.arange(tok)
    flip = row[:, None] // TILE * TILE + TILE - 1 - row[:, None] % TILE == row[None, :]
    local_grad = lag_sums(
        has_after, product, grad_conv, after, mask.astype(jnp.bfloat16),
        flip.astype(jnp.bfloat16), taps,
    )
    taps_f32 = filters.astype(jnp.float32)
    line_bwd = jnp.pad(taps_f32, ((0, 0), (0, LANES - taps)))
    line_fwd = jnp.pad(taps_f32[:, ::-1], ((0, 0), (1, LANES - taps - 1)))
    filter_grad = summed(local_grad)
    mixed_out, grad_query = gated_conv(has_before, line_fwd, product, before, gate_q, cotan, True)
    grad_key, grad_value = gated_conv(has_after, line_bwd, grad_conv, after, feat_v, gate_k, False)
    scale = (lax.axis_size("dp") * size * tok * (channels // groups)) ** (-0.5)
    low, right = low_rank(filter_grad, basis_prev, scale)
    return (mixed_out[None], grad_query[None], grad_key[None], grad_value[None], low, right)


def solution(mesh):
    dp = mesh.shape["dp"]
    fine = Mesh(mesh.devices.reshape(dp, -1, 4, 2), ("dp", "z", "y", "core"))
    split = P("dp", ("z", "y", "core"), None)
    return jax.shard_map(
        on_device,
        mesh=fine,
        in_specs=(split, split, split, P(), split, P()),
        out_specs=(split, split, split, split, P(), P()),
        check_vma=False,
    )
```

```python
import functools

import jax
import jax.numpy as jnp
import numpy as np
from jax import lax
from jax.experimental import pallas as pl
from jax.experimental.pallas import tpu as pltpu
from jax.sharding import Mesh
from jax.sharding import PartitionSpec as P

HIGH = lax.Precision.HIGHEST
LANES = 256
TILE = 16
GROUP = 16
GROUPS = LANES // GROUP
STEP = 1024
NN = (((1,), (0,)), ((), ()))
NT = (((1,), (1,)), ((), ()))
VMEM_LIMIT = 24 * 1024 * 1024


def dot(a, b, dims=NN, precision=None):
    return lax.dot_general(a, b, dims, precision=precision, preferred_element_type=jnp.float32)


def off_chip(x):
    return pltpu.with_memory_space_constraint(x, pltpu.HBM)


def gate_kernel(cotan_ref, query_ref, key_ref, value_ref, grad_ref, prod_ref):
    width = cotan_ref.shape[1]
    cols = pl.ds(pl.multiple_of(pl.program_id(0) * width, width), width)
    for a, b, out in ((cotan_ref, query_ref, grad_ref), (key_ref, value_ref, prod_ref)):
        out[:, cols] = (a[...].astype(jnp.float32) * b[...].astype(jnp.float32)).astype(jnp.bfloat16)


def gated(query, key, value, cotan, grad_half):
    tok, channels = query.shape
    half = channels // 2
    width = STEP
    steps = half // width
    grad_at = pl.BlockSpec((tok, width), lambda i: (0, grad_half * steps + i))
    prod_at = pl.BlockSpec((tok, width), lambda i: (0, (1 - grad_half) * steps + i))
    return pl.pallas_call(
        gate_kernel,
        grid=(steps,),
        in_specs=[grad_at, grad_at, prod_at, prod_at],
        out_specs=[pl.BlockSpec(memory_space=pltpu.VMEM)] * 2,
        out_shape=[jax.ShapeDtypeStruct((tok, half), jnp.bfloat16)] * 2,
        compiler_params=pltpu.CompilerParams(vmem_limit_bytes=VMEM_LIMIT),
        cost_estimate=pl.CostEstimate(
            flops=2 * tok * half, bytes_accessed=12 * tok * half, transcendentals=0
        ),
        name="gated",
    )(*map(off_chip, (cotan, query, key, value)))


def lag_block(rows, window, flip, mask):
    tok = rows.shape[0]
    turned = dot(flip, rows).astype(jnp.bfloat16)
    reach = tok + TILE
    total = jnp.zeros((GROUPS * TILE, reach), jnp.float32)
    for low in range(0, tok, TILE):
        spread = jnp.concatenate([turned[low : low + TILE]] * GROUPS, axis=0) * mask
        total += dot(spread, window[low : low + reach], NT)
    rest = jnp.zeros((GROUPS * TILE, LANES - reach), jnp.float32)
    wide = jnp.concatenate([total, rest], axis=1).reshape(GROUPS, TILE, LANES)
    return jnp.sum(pltpu.roll(wide, 0, 2, stride=1, stride_axis=1), axis=1)


def lag_kernel(
    keep_ref, prod_a, grad_a, after_ref, prod_b, grad_b, before_ref, mask_ref, flip_ref, turn_ref, out_ref
):
    taps = out_ref.shape[1]
    has_before = keep_ref[0].astype(jnp.bfloat16)
    has_after = keep_ref[1].astype(jnp.bfloat16)
    mask, flip = mask_ref[...], flip_ref[...]
    late = []
    for low in range(0, prod_a.shape[1], LANES):
        cols = slice(low, low + LANES)
        window = jnp.concatenate([grad_a[:, cols], after_ref[:, cols] * has_after], axis=0)
        lined = lag_block(prod_a[:, cols], window, flip, mask)
        first = low // GROUP
        out_ref[first : first + GROUPS, :] = pltpu.roll(lined, LANES - TILE + 1, 1)[:, :taps]
        window = jnp.concatenate([before_ref[:, cols] * has_before, prod_b[:, cols]], axis=0)
        late.append(lag_block(grad_b[:, cols], window, flip, mask))
    out_ref[len(late) * GROUPS :, :] = dot(jnp.concatenate(late, axis=0), turn_ref[...], precision=HIGH)


def lag_sums(keep, prod_a, grad_a, after, prod_b, grad_b, before, taps):
    tok, channels = prod_a.shape
    where = np.arange(LANES)
    mask = where[:, None] // TILE == where[None, :] // GROUP
    row = np.arange(tok)
    flip = row[:, None] // TILE * TILE + TILE - 1 - row[:, None] % TILE == row[None, :]
    turn = where[:, None] == tok + TILE - 1 - np.arange(taps)[None, :]
    fixed = [
        jnp.asarray(mask, jnp.bfloat16),
        jnp.asarray(flip, jnp.bfloat16),
        jnp.asarray(turn, jnp.float32),
    ]
    whole = pl.BlockSpec(memory_space=pltpu.VMEM)
    return pl.pallas_call(
        lag_kernel,
        in_specs=[pl.BlockSpec(memory_space=pltpu.SMEM)] + [whole] * (6 + len(fixed)),
        out_specs=whole,
        out_shape=jax.ShapeDtypeStruct((2 * channels // GROUP, taps), jnp.float32),
        compiler_params=pltpu.CompilerParams(vmem_limit_bytes=VMEM_LIMIT),
        cost_estimate=pl.CostEstimate(
            flops=2 * tok * 2 * channels * LANES * 16,
            bytes_accessed=12 * tok * channels,
            transcendentals=0,
        ),
        name="lag_sums",
    )(keep, prod_a, grad_a, after, prod_b, grad_b, before, *fixed)


def conv_block(window, line, shift, gates, outs, cols):
    tok = window.shape[0] // 2
    reach = tok + TILE
    line = line.astype(jnp.float32)
    line = jnp.concatenate([line, jnp.zeros_like(line)], axis=1)
    wide = jnp.broadcast_to(line[:, None, :], (GROUPS, TILE, LANES))
    table = pltpu.roll(wide, shift, 2, stride=1, stride_axis=1)
    table = table.reshape(GROUPS * TILE, LANES)[:, :reach].astype(jnp.bfloat16)
    lane_group = lax.broadcasted_iota(jnp.int32, (TILE, 128), 1) // GROUP
    for low in range(0, tok, TILE):
        full = dot(table, window[low : low + reach])
        rows = slice(low, low + TILE)
        for half in range(LANES // 128):
            conv = None
            for g in range(128 // GROUP):
                row = (half * (128 // GROUP) + g) * TILE
                mine = full[row : row + TILE, half * 128 : half * 128 + 128]
                conv = mine if conv is None else jnp.where(lane_group == g, mine, conv)
            lanes = slice(cols.start + half * 128, cols.start + half * 128 + 128)
            for gate, out in zip(gates, outs):
                out[rows, lanes] = (gate[rows, lanes].astype(jnp.float32) * conv).astype(jnp.bfloat16)


def conv_kernel(
    start, keep_ref, fwd_line, prod_ref, before_ref, query_ref, cotan_ref,
    bwd_line, grad_ref, after_ref, value_ref, key_ref, *refs
):
    mixed, grad_query, grad_key, grad_value = refs[-4:]
    has_before = keep_ref[0].astype(jnp.bfloat16)
    has_after = keep_ref[1].astype(jnp.bfloat16)
    width = query_ref.shape[1]
    step = pl.program_id(0) * width + start
    for low in range(0, width, LANES):
        cols = slice(low, low + LANES)
        here = pl.ds(pl.multiple_of(step + low, LANES), LANES)
        lines = slice(low // GROUP, low // GROUP + GROUPS)
        window = jnp.concatenate([before_ref[:, here] * has_before, prod_ref[:, here]], axis=0)
        conv_block(window, fwd_line[lines], 1, (query_ref, cotan_ref), (mixed, grad_query), cols)
        window = jnp.concatenate([grad_ref[:, here], after_ref[:, here] * has_after], axis=0)
        conv_block(window, bwd_line[lines], 0, (value_ref, key_ref), (grad_key, grad_value), cols)


def gated_convs(keep, taps, turned, prod, before, grad, after, gates, fwd_half, start, count, into):
    tok, channels = gates[0].shape
    half = channels // 2 // STEP
    fwd = fwd_half * half + start
    bwd = (1 - fwd_half) * half + start
    whole = pl.BlockSpec(memory_space=pltpu.VMEM)
    at_fwd = pl.BlockSpec((tok, STEP), lambda i: (0, fwd + i))
    at_bwd = pl.BlockSpec((tok, STEP), lambda i: (0, bwd + i))
    width = taps.shape[1]
    shape = jax.ShapeDtypeStruct((tok, channels), jnp.bfloat16)
    in_specs = [
        pl.BlockSpec(memory_space=pltpu.SMEM),
        pl.BlockSpec((STEP // GROUP, width), lambda i: (fwd + i, 0)), whole, whole, at_fwd, at_fwd,
        pl.BlockSpec((STEP // GROUP, width), lambda i: (bwd + i, 0)), whole, whole, at_bwd, at_bwd,
    ]
    query, key, value, cotan = map(off_chip, gates)
    args = [keep, turned, prod, before, query, cotan, taps, grad, after, value, key]
    aliases = {len(args) + n: n for n in range(len(into))}
    return pl.pallas_call(
        functools.partial(conv_kernel, start * STEP),
        grid=(count,),
        in_specs=in_specs + [pl.BlockSpec(memory_space=pl.ANY)] * len(into),
        out_specs=[at_fwd, at_fwd, at_bwd, at_bwd],
        out_shape=[shape] * 4,
        input_output_aliases=aliases,
        compiler_params=pltpu.CompilerParams(vmem_limit_bytes=VMEM_LIMIT),
        cost_estimate=pl.CostEstimate(
            flops=8 * count * tok * STEP * LANES * 16,
            bytes_accessed=24 * count * tok * STEP,
            transcendentals=0,
        ),
        name="gated_convs",
    )(*args, *into)


def low_rank_kernel(scale, grad_ref, basis_ref, low_ref, next_ref):
    grad = grad_ref[...]
    left = dot(basis_ref[...], grad, NT, HIGH)
    index = lax.broadcasted_iota(jnp.int32, left.shape, 0)
    rest = left
    ortho = jnp.zeros_like(left)
    for i in range(left.shape[0]):
        row = rest[i : i + 1]
        unit = row / jnp.sqrt(jnp.sum(row * row, axis=1, keepdims=True) + 1e-06)
        ortho = jnp.where(index == i, unit, ortho)
        coeff = jnp.sum(left * unit, axis=1, keepdims=True)
        rest = rest - coeff * unit
    right = dot(ortho, grad, NN, HIGH) * scale
    next_ref[...] = right
    low_ref[...] = dot(ortho, right, (((0,), (0,)), ((), ())), HIGH)


def low_rank(grad, basis, scale):
    return pl.pallas_call(
        functools.partial(low_rank_kernel, scale),
        out_shape=[
            jax.ShapeDtypeStruct(grad.shape, jnp.float32),
            jax.ShapeDtypeStruct(basis.shape, jnp.float32),
        ],
        compiler_params=pltpu.CompilerParams(vmem_limit_bytes=VMEM_LIMIT),
        name="low_rank",
    )(grad, basis)


def tie(*arrays):
    return lax.optimization_barrier(arrays)


def on_device(query_gate, key_gate, value_feat, filters, grad_out, basis_prev):
    query, key, value, cotan = query_gate[0], key_gate[0], value_feat[0], grad_out[0]
    tok, channels = query.shape
    groups, taps = filters.shape
    seq = ("z", "y", "core")
    near = ("dp", "y", "core")
    size = lax.axis_size(seq)
    place = lax.axis_index(seq)

    def from_next(x):
        return lax.ppermute(x, seq, [(i, (i - 1) % size) for i in range(size)])

    def from_last(x):
        return lax.ppermute(x, seq, [(i, (i + 1) % size) for i in range(size)])

    gates = (query, key, value, cotan)
    grad_a, prod_b = gated(*gates, 0)
    after_a, before_b = from_next(grad_a), from_last(prod_b)
    grad_b, prod_a = gated(*tie(*gates, grad_a, prod_b)[:4], 1)
    keep = jnp.stack([place > 0, place < size - 1]).astype(jnp.float32)
    turned = filters[:, ::-1]
    local = lag_sums(keep, prod_a, grad_a, after_a, prod_b, grad_b, before_b, taps)

    outs = ()

    def beside(start, given, windows, *which):
        nonlocal outs
        got = start(given)
        windows = tie(*windows, given)[:4]
        outs = gated_convs(keep, filters, turned, *windows, gates, *which, outs)
        got, *outs = tie(got, *outs)
        return got

    count = lax.axis_size(near)

    def exchanged(x):
        return lax.all_to_all(x, near, 0, 0, tiled=True)

    def hop(distance):
        route = [(i, i ^ distance) for i in range(lax.axis_size("z"))]
        return lambda x: lax.ppermute(x, "z", route)

    piece = beside(exchanged, local, (prod_b, before_b, grad_a, after_a), 1, 0, 2)
    piece = piece.reshape(count, groups // count, taps).sum(axis=0)
    grad_b, prod_a, _ = tie(grad_b, prod_a, piece)
    after_b, before_a = from_next(grad_b), from_last(prod_a)
    second = (prod_a, before_a, grad_b, after_b)
    piece = piece + hop(1)(piece)
    piece = piece + hop(2)(piece)
    piece = piece + beside(hop(4), piece, second, 0, 0, 1)
    spread = jnp.broadcast_to(piece[None], (count,) + piece.shape).reshape(groups, taps)
    filter_grad = beside(exchanged, spread, second, 0, 1, 1)
    scale = (lax.axis_size("dp") * size * tok * (channels // groups)) ** (-0.5)
    low, right = low_rank(filter_grad, basis_prev.T, scale)
    return (*[out[None] for out in outs], low, right.T)


def solution(mesh):
    dp = mesh.shape["dp"]
    fine = Mesh(mesh.devices.reshape(dp, -1, 4, 2), ("dp", "z", "y", "core"))
    split = P("dp", ("z", "y", "core"), None)
    return jax.shard_map(
        on_device,
        mesh=fine,
        in_specs=(split, split, split, P(), split, P()),
        out_specs=(split, split, split, split, P(), P()),
        check_vma=False,
    )
```

```python
import functools

import jax
import jax.numpy as jnp
import numpy as np
from jax import lax
from jax.experimental import pallas as pl
from jax.experimental.pallas import tpu as pltpu
from jax.sharding import Mesh
from jax.sharding import PartitionSpec as P

HIGH = lax.Precision.HIGHEST
LANES = 256
TILE = 16
GROUP = 16
GROUPS = LANES // GROUP
STEP = 1024
NN = (((1,), (0,)), ((), ()))
NT = (((1,), (1,)), ((), ()))
VMEM_LIMIT = 24 * 1024 * 1024


def dot(a, b, dims=NN, precision=None):
    return lax.dot_general(a, b, dims, precision=precision, preferred_element_type=jnp.float32)


def off_chip(x):
    return pltpu.with_memory_space_constraint(x, pltpu.HBM)


def gate_kernel(cotan_ref, query_ref, key_ref, value_ref, grad_ref, prod_ref):
    width = cotan_ref.shape[1]
    cols = pl.ds(pl.multiple_of(pl.program_id(0) * width, width), width)
    for a, b, out in ((cotan_ref, query_ref, grad_ref), (key_ref, value_ref, prod_ref)):
        out[:, cols] = (a[...].astype(jnp.float32) * b[...].astype(jnp.float32)).astype(jnp.bfloat16)


def gated(query, key, value, cotan, grad_half):
    tok, channels = query.shape
    half = channels // 2
    width = STEP
    steps = half // width
    grad_at = pl.BlockSpec((tok, width), lambda i: (0, grad_half * steps + i))
    prod_at = pl.BlockSpec((tok, width), lambda i: (0, (1 - grad_half) * steps + i))
    return pl.pallas_call(
        gate_kernel,
        grid=(steps,),
        in_specs=[grad_at, grad_at, prod_at, prod_at],
        out_specs=[pl.BlockSpec(memory_space=pltpu.VMEM)] * 2,
        out_shape=[jax.ShapeDtypeStruct((tok, half), jnp.bfloat16)] * 2,
        compiler_params=pltpu.CompilerParams(vmem_limit_bytes=VMEM_LIMIT),
        cost_estimate=pl.CostEstimate(
            flops=2 * tok * half, bytes_accessed=12 * tok * half, transcendentals=0
        ),
        name="gated",
    )(*map(off_chip, (cotan, query, key, value)))


def lag_block(rows, window, flip, mask):
    tok = rows.shape[0]
    turned = dot(flip, rows).astype(jnp.bfloat16)
    reach = tok + TILE
    total = jnp.zeros((GROUPS * TILE, reach), jnp.float32)
    for low in range(0, tok, TILE):
        spread = jnp.concatenate([turned[low : low + TILE]] * GROUPS, axis=0) * mask
        total += dot(spread, window[low : low + reach], NT)
    rest = jnp.zeros((GROUPS * TILE, LANES - reach), jnp.float32)
    wide = jnp.concatenate([total, rest], axis=1).reshape(GROUPS, TILE, LANES)
    return jnp.sum(pltpu.roll(wide, 0, 2, stride=1, stride_axis=1), axis=1)


def lag_kernel(
    keep_ref, prod_a, grad_a, after_ref, prod_b, grad_b, before_ref, mask_ref, flip_ref, turn_ref, out_ref
):
    taps = out_ref.shape[1]
    has_before = keep_ref[0].astype(jnp.bfloat16)
    has_after = keep_ref[1].astype(jnp.bfloat16)
    mask, flip = mask_ref[...], flip_ref[...]
    late = []
    for low in range(0, prod_a.shape[1], LANES):
        cols = slice(low, low + LANES)
        window = jnp.concatenate([grad_a[:, cols], after_ref[:, cols] * has_after], axis=0)
        lined = lag_block(prod_a[:, cols], window, flip, mask)
        first = low // GROUP
        out_ref[first : first + GROUPS, :] = pltpu.roll(lined, LANES - TILE + 1, 1)[:, :taps]
        window = jnp.concatenate([before_ref[:, cols] * has_before, prod_b[:, cols]], axis=0)
        late.append(lag_block(grad_b[:, cols], window, flip, mask))
    out_ref[len(late) * GROUPS :, :] = dot(jnp.concatenate(late, axis=0), turn_ref[...], precision=HIGH)


def lag_sums(keep, prod_a, grad_a, after, prod_b, grad_b, before, taps):
    tok, channels = prod_a.shape
    where = np.arange(LANES)
    mask = where[:, None] // TILE == where[None, :] // GROUP
    row = np.arange(tok)
    flip = row[:, None] // TILE * TILE + TILE - 1 - row[:, None] % TILE == row[None, :]
    turn = where[:, None] == tok + TILE - 1 - np.arange(taps)[None, :]
    fixed = [
        jnp.asarray(mask, jnp.bfloat16),
        jnp.asarray(flip, jnp.bfloat16),
        jnp.asarray(turn, jnp.float32),
    ]
    whole = pl.BlockSpec(memory_space=pltpu.VMEM)
    return pl.pallas_call(
        lag_kernel,
        in_specs=[pl.BlockSpec(memory_space=pltpu.SMEM)] + [whole] * (6 + len(fixed)),
        out_specs=whole,
        out_shape=jax.ShapeDtypeStruct((2 * channels // GROUP, taps), jnp.float32),
        compiler_params=pltpu.CompilerParams(vmem_limit_bytes=VMEM_LIMIT),
        cost_estimate=pl.CostEstimate(
            flops=2 * tok * 2 * channels * LANES * 16,
            bytes_accessed=12 * tok * channels,
            transcendentals=0,
        ),
        name="lag_sums",
    )(keep, prod_a, grad_a, after, prod_b, grad_b, before, *fixed)


def conv_block(window, line, shift, gates, outs, cols):
    tok = window.shape[0] // 2
    reach = tok + TILE
    line = line.astype(jnp.float32)
    line = jnp.concatenate([line, jnp.zeros_like(line)], axis=1)
    wide = jnp.broadcast_to(line[:, None, :], (GROUPS, TILE, LANES))
    table = pltpu.roll(wide, shift, 2, stride=1, stride_axis=1)
    table = table.reshape(GROUPS * TILE, LANES)[:, :reach].astype(jnp.bfloat16)
    lane_group = lax.broadcasted_iota(jnp.int32, (TILE, 128), 1) // GROUP
    for low in range(0, tok, TILE):
        full = dot(table, window[low : low + reach])
        rows = slice(low, low + TILE)
        for half in range(LANES // 128):
            conv = None
            for g in range(128 // GROUP):
                row = (half * (128 // GROUP) + g) * TILE
                mine = full[row : row + TILE, half * 128 : half * 128 + 128]
                conv = mine if conv is None else jnp.where(lane_group == g, mine, conv)
            lanes = slice(cols.start + half * 128, cols.start + half * 128 + 128)
            for gate, out in zip(gates, outs):
                out[rows, lanes] = (gate[rows, lanes].astype(jnp.float32) * conv).astype(jnp.bfloat16)


def conv_kernel(
    start, blocked, keep_ref, fwd_line, prod_ref, before_ref, query_ref, cotan_ref,
    bwd_line, grad_ref, after_ref, value_ref, key_ref, *refs
):
    mixed, grad_query, grad_key, grad_value = refs[-4:]
    has_before = keep_ref[0].astype(jnp.bfloat16)
    has_after = keep_ref[1].astype(jnp.bfloat16)
    width = query_ref.shape[1]
    step = pl.program_id(0) * width + start
    for low in range(0, width, LANES):
        cols = slice(low, low + LANES)
        here = pl.ds(pl.multiple_of(step + low, LANES), LANES)
        there = cols if blocked else here
        lines = slice(low // GROUP, low // GROUP + GROUPS)
        window = jnp.concatenate([before_ref[:, there] * has_before, prod_ref[:, here]], axis=0)
        conv_block(window, fwd_line[lines], 1, (query_ref, cotan_ref), (mixed, grad_query), cols)
        window = jnp.concatenate([grad_ref[:, here], after_ref[:, there] * has_after], axis=0)
        conv_block(window, bwd_line[lines], 0, (value_ref, key_ref), (grad_key, grad_value), cols)


def gated_convs(keep, taps, turned, prod, before, grad, after, gates, fwd_half, start, count, blocked, into):
    tok, channels = gates[0].shape
    half = channels // 2 // STEP
    fwd = fwd_half * half + start
    bwd = (1 - fwd_half) * half + start
    whole = pl.BlockSpec(memory_space=pltpu.VMEM)
    at_fwd = pl.BlockSpec((tok, STEP), lambda i: (0, fwd + i))
    at_bwd = pl.BlockSpec((tok, STEP), lambda i: (0, bwd + i))
    halo = pl.BlockSpec((tok, STEP), lambda i: (0, start + i)) if blocked else whole
    if blocked:
        before, after = off_chip(before), off_chip(after)
    width = taps.shape[1]
    shape = jax.ShapeDtypeStruct((tok, channels), jnp.bfloat16)
    in_specs = [
        pl.BlockSpec(memory_space=pltpu.SMEM),
        pl.BlockSpec((STEP // GROUP, width), lambda i: (fwd + i, 0)), whole, halo, at_fwd, at_fwd,
        pl.BlockSpec((STEP // GROUP, width), lambda i: (bwd + i, 0)), whole, halo, at_bwd, at_bwd,
    ]
    query, key, value, cotan = map(off_chip, gates)
    args = [keep, turned, prod, before, query, cotan, taps, grad, after, value, key]
    aliases = {len(args) + n: n for n in range(len(into))}
    return pl.pallas_call(
        functools.partial(conv_kernel, start * STEP, blocked),
        grid=(count,),
        in_specs=in_specs + [pl.BlockSpec(memory_space=pl.ANY)] * len(into),
        out_specs=[at_fwd, at_fwd, at_bwd, at_bwd],
        out_shape=[shape] * 4,
        input_output_aliases=aliases,
        compiler_params=pltpu.CompilerParams(vmem_limit_bytes=VMEM_LIMIT),
        cost_estimate=pl.CostEstimate(
            flops=8 * count * tok * STEP * LANES * 16,
            bytes_accessed=24 * count * tok * STEP,
            transcendentals=0,
        ),
        name="gated_convs",
    )(*args, *into)


def low_rank_kernel(scale, grad_ref, basis_ref, low_ref, next_ref):
    grad = grad_ref[...]
    left = dot(basis_ref[...], grad, NT, HIGH)
    index = lax.broadcasted_iota(jnp.int32, left.shape, 0)
    rest = left
    ortho = jnp.zeros_like(left)
    for i in range(left.shape[0]):
        row = rest[i : i + 1]
        square = jnp.sum(row * row, axis=1, keepdims=True) + 1e-06
        coeff = jnp.sum(left * row, axis=1, keepdims=True)
        ortho = jnp.where(index == i, row / jnp.sqrt(square), ortho)
        rest = rest - (coeff / square) * row
    right = dot(ortho, grad, NN, HIGH) * scale
    next_ref[...] = right
    low_ref[...] = dot(ortho, right, (((0,), (0,)), ((), ())), HIGH)


def low_rank(grad, basis, scale):
    return pl.pallas_call(
        functools.partial(low_rank_kernel, scale),
        out_shape=[
            jax.ShapeDtypeStruct(grad.shape, jnp.float32),
            jax.ShapeDtypeStruct(basis.shape, jnp.float32),
        ],
        compiler_params=pltpu.CompilerParams(vmem_limit_bytes=VMEM_LIMIT),
        name="low_rank",
    )(grad, basis)


def tie(*arrays):
    return lax.optimization_barrier(arrays)


def on_device(query_gate, key_gate, value_feat, filters, grad_out, basis_prev):
    query, key, value, cotan = query_gate[0], key_gate[0], value_feat[0], grad_out[0]
    tok, channels = query.shape
    groups, taps = filters.shape
    seq = ("z", "y", "core")
    near = ("dp", "y", "core")
    size = lax.axis_size(seq)
    place = lax.axis_index(seq)

    def from_next(x):
        return lax.ppermute(x, seq, [(i, (i - 1) % size) for i in range(size)])

    def from_last(x):
        return lax.ppermute(x, seq, [(i, (i + 1) % size) for i in range(size)])

    gates = (query, key, value, cotan)
    grad_a, prod_b = gated(*gates, 0)
    after_a, before_b = from_next(grad_a), from_last(prod_b)
    grad_b, prod_a = gated(*tie(*gates, grad_a, prod_b)[:4], 1)
    keep = jnp.stack([place > 0, place < size - 1]).astype(jnp.float32)
    turned = filters[:, ::-1]
    local = lag_sums(keep, prod_a, grad_a, after_a, prod_b, grad_b, before_b, taps)

    outs = ()

    def beside(start, given, windows, *which):
        nonlocal outs
        got = start(given)
        now, _ = tie(keep, given)
        outs = gated_convs(now, filters, turned, *windows, gates, *which, outs)
        got, *outs = tie(got, *outs)
        return got

    count = lax.axis_size(near)

    def exchanged(x):
        return lax.all_to_all(x, near, 0, 0, tiled=True)

    def hop(distance):
        route = [(i, i ^ distance) for i in range(lax.axis_size("z"))]
        return lambda x: lax.ppermute(x, "z", route)

    grad_b, prod_a, local = tie(grad_b, prod_a, local)
    after_b, before_a = from_next(grad_b), from_last(prod_a)
    second = (prod_a, before_a, grad_b, after_b)
    first = (prod_b, before_b, grad_a, after_a)
    piece = beside(exchanged, local, first, 1, 0, 1, False)
    piece = piece.reshape(count, groups // count, taps).sum(axis=0)
    piece = piece + beside(hop(1), piece, first, 1, 1, 1, False)
    piece = piece + hop(2)(piece)
    piece = piece + beside(hop(4), piece, second, 0, 0, 1, True)
    spread = jnp.broadcast_to(piece[None], (count,) + piece.shape).reshape(groups, taps)
    filter_grad = beside(exchanged, spread, second, 0, 1, 1, True)
    scale = (lax.axis_size("dp") * size * tok * (channels // groups)) ** (-0.5)
    low, right = low_rank(filter_grad, basis_prev.T, scale)
    return (*[out[None] for out in outs], low, right.T)


def solution(mesh):
    dp = mesh.shape["dp"]
    fine = Mesh(mesh.devices.reshape(dp, -1, 4, 2), ("dp", "z", "y", "core"))
    split = P("dp", ("z", "y", "core"), None)
    return jax.shard_map(
        on_device,
        mesh=fine,
        in_specs=(split, split, split, P(), split, P()),
        out_specs=(split, split, split, split, P(), P()),
        check_vma=False,
    )
```

```python
import functools

import jax
import jax.numpy as jnp
import numpy as np
from jax import lax
from jax.experimental import pallas as pl
from jax.experimental.pallas import tpu as pltpu
from jax.sharding import Mesh
from jax.sharding import PartitionSpec as P

HIGH = lax.Precision.HIGHEST
LANES = 256
TILE = 16
GROUP = 16
GROUPS = LANES // GROUP
STEP = 1024
NN = (((1,), (0,)), ((), ()))
NT = (((1,), (1,)), ((), ()))
VMEM_LIMIT = 24 * 1024 * 1024


def dot(a, b, dims=NN, precision=None):
    return lax.dot_general(a, b, dims, precision=precision, preferred_element_type=jnp.float32)


def off_chip(x):
    return pltpu.with_memory_space_constraint(x, pltpu.HBM)


def gate_kernel(cotan_ref, query_ref, key_ref, value_ref, grad_ref, prod_ref):
    width = cotan_ref.shape[1]
    cols = pl.ds(pl.multiple_of(pl.program_id(0) * width, width), width)
    for a, b, out in ((cotan_ref, query_ref, grad_ref), (key_ref, value_ref, prod_ref)):
        out[:, cols] = (a[...].astype(jnp.float32) * b[...].astype(jnp.float32)).astype(jnp.bfloat16)


def gated(query, key, value, cotan, grad_half):
    tok, channels = query.shape
    half = channels // 2
    width = STEP
    steps = half // width
    grad_at = pl.BlockSpec((tok, width), lambda i: (0, grad_half * steps + i))
    prod_at = pl.BlockSpec((tok, width), lambda i: (0, (1 - grad_half) * steps + i))
    return pl.pallas_call(
        gate_kernel,
        grid=(steps,),
        in_specs=[grad_at, grad_at, prod_at, prod_at],
        out_specs=[pl.BlockSpec(memory_space=pltpu.VMEM)] * 2,
        out_shape=[jax.ShapeDtypeStruct((tok, half), jnp.bfloat16)] * 2,
        compiler_params=pltpu.CompilerParams(vmem_limit_bytes=VMEM_LIMIT),
        cost_estimate=pl.CostEstimate(
            flops=2 * tok * half, bytes_accessed=12 * tok * half, transcendentals=0
        ),
        name="gated",
    )(*map(off_chip, (cotan, query, key, value)))


def lag_block(rows, window, flip, mask):
    tok = rows.shape[0]
    turned = dot(flip, rows).astype(jnp.bfloat16)
    reach = tok + TILE
    total = jnp.zeros((GROUPS * TILE, reach), jnp.float32)
    for low in range(0, tok, TILE):
        spread = jnp.concatenate([turned[low : low + TILE]] * GROUPS, axis=0) * mask
        total += dot(spread, window[low : low + reach], NT)
    rest = jnp.zeros((GROUPS * TILE, LANES - reach), jnp.float32)
    wide = jnp.concatenate([total, rest], axis=1).reshape(GROUPS, TILE, LANES)
    return jnp.sum(pltpu.roll(wide, 0, 2, stride=1, stride_axis=1), axis=1)


def lag_kernel(
    keep_ref, prod_b, grad_b, before_ref, prod_a, grad_a, after_ref, mask_ref, flip_ref, turn_ref, out_ref
):
    taps = out_ref.shape[1]
    has_before = keep_ref[0].astype(jnp.bfloat16)
    has_after = keep_ref[1].astype(jnp.bfloat16)
    mask, flip = mask_ref[...], flip_ref[...]
    late = []
    for low in range(0, prod_a.shape[1], LANES):
        cols = slice(low, low + LANES)
        window = jnp.concatenate([grad_a[:, cols], after_ref[:, cols] * has_after], axis=0)
        lined = lag_block(prod_a[:, cols], window, flip, mask)
        first = low // GROUP
        out_ref[first : first + GROUPS, :] = pltpu.roll(lined, LANES - TILE + 1, 1)[:, :taps]
        window = jnp.concatenate([before_ref[:, cols] * has_before, prod_b[:, cols]], axis=0)
        late.append(lag_block(grad_b[:, cols], window, flip, mask))
    out_ref[len(late) * GROUPS :, :] = dot(jnp.concatenate(late, axis=0), turn_ref[...], precision=HIGH)


def lag_sums(keep, prod_a, grad_a, after, prod_b, grad_b, before, taps):
    tok, channels = prod_a.shape
    where = np.arange(LANES)
    mask = where[:, None] // TILE == where[None, :] // GROUP
    row = np.arange(tok)
    flip = row[:, None] // TILE * TILE + TILE - 1 - row[:, None] % TILE == row[None, :]
    turn = where[:, None] == tok + TILE - 1 - np.arange(taps)[None, :]
    fixed = [
        jnp.asarray(mask, jnp.bfloat16),
        jnp.asarray(flip, jnp.bfloat16),
        jnp.asarray(turn, jnp.float32),
    ]
    whole = pl.BlockSpec(memory_space=pltpu.VMEM)
    return pl.pallas_call(
        lag_kernel,
        in_specs=[pl.BlockSpec(memory_space=pltpu.SMEM)] + [whole] * (6 + len(fixed)),
        out_specs=whole,
        out_shape=jax.ShapeDtypeStruct((2 * channels // GROUP, taps), jnp.float32),
        compiler_params=pltpu.CompilerParams(vmem_limit_bytes=VMEM_LIMIT),
        cost_estimate=pl.CostEstimate(
            flops=2 * tok * 2 * channels * LANES * 16,
            bytes_accessed=12 * tok * channels,
            transcendentals=0,
        ),
        name="lag_sums",
    )(keep, prod_b, grad_b, before, prod_a, grad_a, after, *fixed)


def conv_block(window, line, shift, gates, outs, cols):
    tok = window.shape[0] // 2
    reach = tok + TILE
    line = line.astype(jnp.float32)
    line = jnp.concatenate([line, jnp.zeros_like(line)], axis=1)
    wide = jnp.broadcast_to(line[:, None, :], (GROUPS, TILE, LANES))
    table = pltpu.roll(wide, shift, 2, stride=1, stride_axis=1)
    table = table.reshape(GROUPS * TILE, LANES)[:, :reach].astype(jnp.bfloat16)
    lane_group = lax.broadcasted_iota(jnp.int32, (TILE, 128), 1) // GROUP
    for low in range(0, tok, TILE):
        full = dot(table, window[low : low + reach])
        rows = slice(low, low + TILE)
        for half in range(LANES // 128):
            conv = None
            for g in range(128 // GROUP):
                row = (half * (128 // GROUP) + g) * TILE
                mine = full[row : row + TILE, half * 128 : half * 128 + 128]
                conv = mine if conv is None else jnp.where(lane_group == g, mine, conv)
            lanes = slice(cols.start + half * 128, cols.start + half * 128 + 128)
            for gate, out in zip(gates, outs):
                out[rows, lanes] = (gate[rows, lanes].astype(jnp.float32) * conv).astype(jnp.bfloat16)


def conv_kernel(
    start, blocked, keep_ref, fwd_line, prod_ref, before_ref, query_ref, cotan_ref,
    bwd_line, grad_ref, after_ref, value_ref, key_ref, *refs
):
    mixed, grad_query, grad_key, grad_value = refs[-4:]
    has_before = keep_ref[0].astype(jnp.bfloat16)
    has_after = keep_ref[1].astype(jnp.bfloat16)
    width = query_ref.shape[1]
    step = pl.program_id(0) * width + start
    for low in range(0, width, LANES):
        cols = slice(low, low + LANES)
        here = pl.ds(pl.multiple_of(step + low, LANES), LANES)
        there = cols if blocked else here
        lines = slice(low // GROUP, low // GROUP + GROUPS)
        window = jnp.concatenate([before_ref[:, there] * has_before, prod_ref[:, here]], axis=0)
        conv_block(window, fwd_line[lines], 1, (query_ref, cotan_ref), (mixed, grad_query), cols)
        window = jnp.concatenate([grad_ref[:, here], after_ref[:, there] * has_after], axis=0)
        conv_block(window, bwd_line[lines], 0, (value_ref, key_ref), (grad_key, grad_value), cols)


def gated_convs(keep, taps, turned, prod, before, grad, after, gates, fwd_half, start, count, blocked, into):
    tok, channels = gates[0].shape
    half = channels // 2 // STEP
    fwd = fwd_half * half + start
    bwd = (1 - fwd_half) * half + start
    whole = pl.BlockSpec(memory_space=pltpu.VMEM)
    at_fwd = pl.BlockSpec((tok, STEP), lambda i: (0, fwd + i))
    at_bwd = pl.BlockSpec((tok, STEP), lambda i: (0, bwd + i))
    halo = pl.BlockSpec((tok, STEP), lambda i: (0, start + i)) if blocked else whole
    if blocked:
        before, after = off_chip(before), off_chip(after)
    width = taps.shape[1]
    shape = jax.ShapeDtypeStruct((tok, channels), jnp.bfloat16)
    in_specs = [
        pl.BlockSpec(memory_space=pltpu.SMEM),
        pl.BlockSpec((STEP // GROUP, width), lambda i: (fwd + i, 0)), whole, halo, at_fwd, at_fwd,
        pl.BlockSpec((STEP // GROUP, width), lambda i: (bwd + i, 0)), whole, halo, at_bwd, at_bwd,
    ]
    query, key, value, cotan = map(off_chip, gates)
    args = [keep, turned, prod, before, query, cotan, taps, grad, after, value, key]
    aliases = {len(args) + n: n for n in range(len(into))}
    return pl.pallas_call(
        functools.partial(conv_kernel, start * STEP, blocked),
        grid=(count,),
        in_specs=in_specs + [pl.BlockSpec(memory_space=pl.ANY)] * len(into),
        out_specs=[at_fwd, at_fwd, at_bwd, at_bwd],
        out_shape=[shape] * 4,
        input_output_aliases=aliases,
        compiler_params=pltpu.CompilerParams(vmem_limit_bytes=VMEM_LIMIT),
        cost_estimate=pl.CostEstimate(
            flops=8 * count * tok * STEP * LANES * 16,
            bytes_accessed=24 * count * tok * STEP,
            transcendentals=0,
        ),
        name="gated_convs",
    )(*args, *into)


def low_rank_kernel(scale, grad_ref, basis_ref, low_ref, next_ref):
    grad = grad_ref[...]
    left = dot(basis_ref[...], grad, NT, HIGH)
    index = lax.broadcasted_iota(jnp.int32, left.shape, 0)
    rest = left
    ortho = jnp.zeros_like(left)
    for i in range(left.shape[0]):
        row = rest[i : i + 1]
        square = jnp.sum(row * row, axis=1, keepdims=True) + 1e-06
        coeff = jnp.sum(left * row, axis=1, keepdims=True)
        ortho = jnp.where(index == i, row / jnp.sqrt(square), ortho)
        rest = rest - (coeff / square) * row
    right = dot(ortho, grad, NN, HIGH) * scale
    next_ref[...] = right
    low_ref[...] = dot(ortho, right, (((0,), (0,)), ((), ())), HIGH)


def low_rank(grad, basis, scale):
    return pl.pallas_call(
        functools.partial(low_rank_kernel, scale),
        out_shape=[
            jax.ShapeDtypeStruct(grad.shape, jnp.float32),
            jax.ShapeDtypeStruct(basis.shape, jnp.float32),
        ],
        compiler_params=pltpu.CompilerParams(vmem_limit_bytes=VMEM_LIMIT),
        name="low_rank",
    )(grad, basis)


def tie(*arrays):
    return lax.optimization_barrier(arrays)


def on_device(query_gate, key_gate, value_feat, filters, grad_out, basis_prev):
    query, key, value, cotan = query_gate[0], key_gate[0], value_feat[0], grad_out[0]
    tok, channels = query.shape
    groups, taps = filters.shape
    seq = ("z", "y", "core")
    near = ("dp", "y", "core")
    size = lax.axis_size(seq)
    place = lax.axis_index(seq)

    def from_next(x):
        return lax.ppermute(x, seq, [(i, (i - 1) % size) for i in range(size)])

    def from_last(x):
        return lax.ppermute(x, seq, [(i, (i + 1) % size) for i in range(size)])

    gates = (query, key, value, cotan)
    grad_a, prod_b = gated(*gates, 0)
    after_a, before_b = from_next(grad_a), from_last(prod_b)
    grad_b, prod_a = gated(*tie(*gates, grad_a, prod_b)[:4], 1)
    keep = jnp.stack([place > 0, place < size - 1]).astype(jnp.float32)
    turned = filters[:, ::-1]
    local = lag_sums(keep, prod_a, grad_a, after_a, prod_b, grad_b, before_b, taps)

    outs = ()

    def beside(start, given, windows, *which):
        nonlocal outs
        got = start(given)
        now, _ = tie(keep, given)
        outs = gated_convs(now, filters, turned, *windows, gates, *which, outs)
        got, *outs = tie(got, *outs)
        return got

    count = lax.axis_size(near)

    def exchanged(x):
        return lax.all_to_all(x, near, 0, 0, tiled=True)

    def hop(distance):
        route = [(i, i ^ distance) for i in range(lax.axis_size("z"))]
        return lambda x: lax.ppermute(x, "z", route)

    grad_b, prod_a, local = tie(grad_b, prod_a, local)
    after_b, before_a = from_next(grad_b), from_last(prod_a)
    second = (prod_a, before_a, grad_b, after_b)
    first = (prod_b, before_b, grad_a, after_a)
    piece = beside(exchanged, local, first, 1, 0, 1, False)
    piece = piece.reshape(count, groups // count, taps).sum(axis=0)
    piece = piece + beside(hop(1), piece, first, 1, 1, 1, False)
    piece = piece + hop(2)(piece)
    piece = piece + beside(hop(4), piece, second, 0, 0, 1, True)
    spread = jnp.broadcast_to(piece[None], (count,) + piece.shape).reshape(groups, taps)
    filter_grad = beside(exchanged, spread, second, 0, 1, 1, True)
    scale = (lax.axis_size("dp") * size * tok * (channels // groups)) ** (-0.5)
    low, right = low_rank(filter_grad, basis_prev.T, scale)
    return (*[out[None] for out in outs], low, right.T)


def solution(mesh):
    dp = mesh.shape["dp"]
    fine = Mesh(mesh.devices.reshape(dp, -1, 4, 2), ("dp", "z", "y", "core"))
    split = P("dp", ("z", "y", "core"), None)
    return jax.shard_map(
        on_device,
        mesh=fine,
        in_specs=(split, split, split, P(), split, P()),
        out_specs=(split, split, split, split, P(), P()),
        check_vma=False,
    )
```

```python
import functools

import jax
import jax.numpy as jnp
import numpy as np
from jax import lax
from jax.experimental import pallas as pl
from jax.experimental.pallas import tpu as pltpu
from jax.sharding import Mesh
from jax.sharding import PartitionSpec as P

HIGH = lax.Precision.HIGHEST
LANES = 256
TILE = 16
GROUP = 16
GROUPS = LANES // GROUP
STEP = 1024
NN = (((1,), (0,)), ((), ()))
NT = (((1,), (1,)), ((), ()))
VMEM_LIMIT = 24 * 1024 * 1024


def dot(a, b, dims=NN, precision=None):
    return lax.dot_general(a, b, dims, precision=precision, preferred_element_type=jnp.float32)


def off_chip(x):
    return pltpu.with_memory_space_constraint(x, pltpu.HBM)


def gate_kernel(cotan_ref, query_ref, key_ref, value_ref, grad_ref, prod_ref):
    width = cotan_ref.shape[1]
    cols = pl.ds(pl.multiple_of(pl.program_id(0) * width, width), width)
    for a, b, out in ((cotan_ref, query_ref, grad_ref), (key_ref, value_ref, prod_ref)):
        out[:, cols] = (a[...].astype(jnp.float32) * b[...].astype(jnp.float32)).astype(jnp.bfloat16)


def gated(query, key, value, cotan, grad_half):
    tok, channels = query.shape
    half = channels // 2
    width = STEP
    steps = half // width
    grad_at = pl.BlockSpec((tok, width), lambda i: (0, grad_half * steps + i))
    prod_at = pl.BlockSpec((tok, width), lambda i: (0, (1 - grad_half) * steps + i))
    return pl.pallas_call(
        gate_kernel,
        grid=(steps,),
        in_specs=[grad_at, grad_at, prod_at, prod_at],
        out_specs=[pl.BlockSpec(memory_space=pltpu.VMEM)] * 2,
        out_shape=[jax.ShapeDtypeStruct((tok, half), jnp.bfloat16)] * 2,
        compiler_params=pltpu.CompilerParams(vmem_limit_bytes=VMEM_LIMIT),
        cost_estimate=pl.CostEstimate(
            flops=2 * tok * half, bytes_accessed=12 * tok * half, transcendentals=0
        ),
        name="gated",
    )(*map(off_chip, (cotan, query, key, value)))


def lag_block(rows, window, flip, mask):
    tok = rows.shape[0]
    turned = dot(flip, rows).astype(jnp.bfloat16)
    reach = tok + TILE
    total = jnp.zeros((GROUPS * TILE, reach), jnp.float32)
    for low in range(0, tok, TILE):
        spread = jnp.concatenate([turned[low : low + TILE]] * GROUPS, axis=0) * mask
        total += dot(spread, window[low : low + reach], NT)
    rest = jnp.zeros((GROUPS * TILE, LANES - reach), jnp.float32)
    wide = jnp.concatenate([total, rest], axis=1).reshape(GROUPS, TILE, LANES)
    return jnp.sum(pltpu.roll(wide, 0, 2, stride=1, stride_axis=1), axis=1)


def lag_kernel(
    keep_ref, prod_b, grad_b, before_ref, prod_a, grad_a, after_ref, mask_ref, flip_ref, turn_ref, out_ref
):
    taps = out_ref.shape[1]
    has_before = keep_ref[0].astype(jnp.bfloat16)
    has_after = keep_ref[1].astype(jnp.bfloat16)
    mask, flip = mask_ref[...], flip_ref[...]
    late = []
    for low in range(0, prod_a.shape[1], LANES):
        cols = slice(low, low + LANES)
        window = jnp.concatenate([grad_a[:, cols], after_ref[:, cols] * has_after], axis=0)
        lined = lag_block(prod_a[:, cols], window, flip, mask)
        first = low // GROUP
        out_ref[first : first + GROUPS, :] = pltpu.roll(lined, LANES - TILE + 1, 1)[:, :taps]
        window = jnp.concatenate([before_ref[:, cols] * has_before, prod_b[:, cols]], axis=0)
        late.append(lag_block(grad_b[:, cols], window, flip, mask))
    out_ref[len(late) * GROUPS :, :] = dot(jnp.concatenate(late, axis=0), turn_ref[...], precision=HIGH)


def lag_sums(keep, prod_a, grad_a, after, prod_b, grad_b, before, taps):
    tok, channels = prod_a.shape
    where = np.arange(LANES)
    mask = where[:, None] // TILE == where[None, :] // GROUP
    row = np.arange(tok)
    flip = row[:, None] // TILE * TILE + TILE - 1 - row[:, None] % TILE == row[None, :]
    turn = where[:, None] == tok + TILE - 1 - np.arange(taps)[None, :]
    fixed = [
        jnp.asarray(mask, jnp.bfloat16),
        jnp.asarray(flip, jnp.bfloat16),
        jnp.asarray(turn, jnp.float32),
    ]
    whole = pl.BlockSpec(memory_space=pltpu.VMEM)
    return pl.pallas_call(
        lag_kernel,
        in_specs=[pl.BlockSpec(memory_space=pltpu.SMEM)] + [whole] * (6 + len(fixed)),
        out_specs=whole,
        out_shape=jax.ShapeDtypeStruct((2 * channels // GROUP, taps), jnp.float32),
        compiler_params=pltpu.CompilerParams(vmem_limit_bytes=VMEM_LIMIT),
        cost_estimate=pl.CostEstimate(
            flops=2 * tok * 2 * channels * LANES * 16,
            bytes_accessed=12 * tok * channels,
            transcendentals=0,
        ),
        name="lag_sums",
    )(keep, prod_b, grad_b, before, prod_a, grad_a, after, *fixed)


def conv_block(window, line, shift, gates, outs, cols):
    tok = window.shape[0] // 2
    reach = tok + TILE
    line = line.astype(jnp.float32)
    line = jnp.concatenate([line, jnp.zeros_like(line)], axis=1)
    wide = jnp.broadcast_to(line[:, None, :], (GROUPS, TILE, LANES))
    table = pltpu.roll(wide, shift, 2, stride=1, stride_axis=1)
    table = table.reshape(GROUPS * TILE, LANES)[:, :reach].astype(jnp.bfloat16)
    lane_group = lax.broadcasted_iota(jnp.int32, (TILE, 128), 1) // GROUP
    for low in range(0, tok, TILE):
        full = dot(table, window[low : low + reach])
        rows = slice(low, low + TILE)
        for half in range(LANES // 128):
            conv = None
            for g in range(128 // GROUP):
                row = (half * (128 // GROUP) + g) * TILE
                mine = full[row : row + TILE, half * 128 : half * 128 + 128]
                conv = mine if conv is None else jnp.where(lane_group == g, mine, conv)
            lanes = slice(cols.start + half * 128, cols.start + half * 128 + 128)
            for gate, out in zip(gates, outs):
                out[rows, lanes] = (gate[rows, lanes].astype(jnp.float32) * conv).astype(jnp.bfloat16)


def conv_kernel(
    start, blocked, keep_ref, fwd_line, prod_ref, before_ref, query_ref, cotan_ref,
    bwd_line, grad_ref, after_ref, value_ref, key_ref, *refs
):
    mixed, grad_query, grad_key, grad_value = refs[-4:]
    has_before = keep_ref[0].astype(jnp.bfloat16)
    has_after = keep_ref[1].astype(jnp.bfloat16)
    width = query_ref.shape[1]
    step = pl.program_id(0) * width + start
    for low in range(0, width, LANES):
        cols = slice(low, low + LANES)
        here = pl.ds(pl.multiple_of(step + low, LANES), LANES)
        there = cols if blocked else here
        lines = slice(low // GROUP, low // GROUP + GROUPS)
        window = jnp.concatenate([before_ref[:, there] * has_before, prod_ref[:, here]], axis=0)
        conv_block(window, fwd_line[lines], 1, (query_ref, cotan_ref), (mixed, grad_query), cols)
        window = jnp.concatenate([grad_ref[:, here], after_ref[:, there] * has_after], axis=0)
        conv_block(window, bwd_line[lines], 0, (value_ref, key_ref), (grad_key, grad_value), cols)


def gated_convs(keep, taps, turned, prod, before, grad, after, gates, fwd_half, start, count, blocked, into):
    tok, channels = gates[0].shape
    half = channels // 2 // STEP
    fwd = fwd_half * half + start
    bwd = (1 - fwd_half) * half + start
    whole = pl.BlockSpec(memory_space=pltpu.VMEM)
    at_fwd = pl.BlockSpec((tok, STEP), lambda i: (0, fwd + i))
    at_bwd = pl.BlockSpec((tok, STEP), lambda i: (0, bwd + i))
    halo = pl.BlockSpec((tok, STEP), lambda i: (0, start + i)) if blocked else whole
    if blocked:
        before, after = off_chip(before), off_chip(after)
    width = taps.shape[1]
    shape = jax.ShapeDtypeStruct((tok, channels), jnp.bfloat16)
    in_specs = [
        pl.BlockSpec(memory_space=pltpu.SMEM),
        pl.BlockSpec((STEP // GROUP, width), lambda i: (fwd + i, 0)), whole, halo, at_fwd, at_fwd,
        pl.BlockSpec((STEP // GROUP, width), lambda i: (bwd + i, 0)), whole, halo, at_bwd, at_bwd,
    ]
    query, key, value, cotan = map(off_chip, gates)
    args = [keep, turned, prod, before, query, cotan, taps, grad, after, value, key]
    aliases = {len(args) + n: n for n in range(len(into))}
    return pl.pallas_call(
        functools.partial(conv_kernel, start * STEP, blocked),
        grid=(count,),
        in_specs=in_specs + [pl.BlockSpec(memory_space=pl.ANY)] * len(into),
        out_specs=[at_fwd, at_fwd, at_bwd, at_bwd],
        out_shape=[shape] * 4,
        input_output_aliases=aliases,
        compiler_params=pltpu.CompilerParams(vmem_limit_bytes=VMEM_LIMIT),
        cost_estimate=pl.CostEstimate(
            flops=8 * count * tok * STEP * LANES * 16,
            bytes_accessed=24 * count * tok * STEP,
            transcendentals=0,
        ),
        name="gated_convs",
    )(*args, *into)


def low_rank_kernel(scale, grad_ref, basis_ref, low_ref, next_ref):
    grad = grad_ref[...]
    left = dot(basis_ref[...], grad, NT, HIGH)
    index = lax.broadcasted_iota(jnp.int32, left.shape, 0)
    rest = left
    ortho = jnp.zeros_like(left)
    for i in range(left.shape[0]):
        row = rest[i : i + 1]
        square = jnp.sum(row * row, axis=1, keepdims=True) + 1e-06
        coeff = jnp.sum(left * row, axis=1, keepdims=True)
        ortho = jnp.where(index == i, row / jnp.sqrt(square), ortho)
        rest = rest - (coeff / square) * row
    right = dot(ortho, grad, NN, HIGH) * scale
    next_ref[...] = right
    low_ref[...] = dot(ortho, right, (((0,), (0,)), ((), ())), HIGH)


def low_rank(grad, basis, scale):
    return pl.pallas_call(
        functools.partial(low_rank_kernel, scale),
        out_shape=[
            jax.ShapeDtypeStruct(grad.shape, jnp.float32),
            jax.ShapeDtypeStruct(basis.shape, jnp.float32),
        ],
        compiler_params=pltpu.CompilerParams(vmem_limit_bytes=VMEM_LIMIT),
        name="low_rank",
    )(grad, off_chip(basis))


def tie(*arrays):
    return lax.optimization_barrier(arrays)


def on_device(query_gate, key_gate, value_feat, filters, grad_out, basis_prev):
    query, key, value, cotan = query_gate[0], key_gate[0], value_feat[0], grad_out[0]
    tok, channels = query.shape
    groups, taps = filters.shape
    seq = ("z", "y", "core")
    near = ("dp", "y", "core")
    size = lax.axis_size(seq)
    place = lax.axis_index(seq)

    def from_next(x):
        return lax.ppermute(x, seq, [(i, (i - 1) % size) for i in range(size)])

    def from_last(x):
        return lax.ppermute(x, seq, [(i, (i + 1) % size) for i in range(size)])

    gates = (query, key, value, cotan)
    grad_a, prod_b = gated(*gates, 0)
    after_a, before_b = from_next(grad_a), from_last(prod_b)
    grad_b, prod_a = gated(*tie(*gates, grad_a, prod_b)[:4], 1)
    keep = jnp.stack([place > 0, place < size - 1]).astype(jnp.float32)
    turned = filters[:, ::-1]
    local = lag_sums(keep, prod_a, grad_a, after_a, prod_b, grad_b, before_b, taps)

    outs = ()

    def beside(start, given, windows, *which):
        nonlocal outs
        got = start(given)
        now, _ = tie(keep, given)
        outs = gated_convs(now, filters, turned, *windows, gates, *which, outs)
        got, *outs = tie(got, *outs)
        return got

    count = lax.axis_size(near)

    def exchanged(x):
        return lax.all_to_all(x, near, 0, 0, tiled=True)

    def hop(distance):
        route = [(i, i ^ distance) for i in range(lax.axis_size("z"))]
        return lambda x: lax.ppermute(x, "z", route)

    grad_b, prod_a, local = tie(grad_b, prod_a, local)
    after_b, before_a = from_next(grad_b), from_last(prod_a)
    second = (prod_a, before_a, grad_b, after_b)
    first = (prod_b, before_b, grad_a, after_a)
    piece = beside(exchanged, local, first, 1, 0, 1, False)
    piece = piece.reshape(count, groups // count, taps).sum(axis=0)
    piece = piece + beside(hop(1), piece, first, 1, 1, 1, False)
    piece = piece + hop(2)(piece)
    piece = piece + beside(hop(4), piece, second, 0, 0, 1, True)
    spread = jnp.broadcast_to(piece[None], (count,) + piece.shape).reshape(groups, taps)
    filter_grad = beside(exchanged, spread, second, 0, 1, 1, True)
    scale = (lax.axis_size("dp") * size * tok * (channels // groups)) ** (-0.5)
    low, right = low_rank(filter_grad, basis_prev.T, scale)
    return (*[out[None] for out in outs], low, right.T)


def solution(mesh):
    dp = mesh.shape["dp"]
    fine = Mesh(mesh.devices.reshape(dp, -1, 4, 2), ("dp", "z", "y", "core"))
    split = P("dp", ("z", "y", "core"), None)
    return jax.shard_map(
        on_device,
        mesh=fine,
        in_specs=(split, split, split, P(), split, P()),
        out_specs=(split, split, split, split, P(), P()),
        check_vma=False,
    )
```
